256 devices in a mesh: row: 4 (over y), col: 16 (over x, z_hi), rep: 4 (over z_lo, core).
Axes of the slice: x: 4, y: 4, z: 8 (z_hi: 4, z_lo: 2; z = z_hi * 2 + z_lo), core: 2. Of those that a mesh axis runs over, the one named last changes fastest.
Arguments:
- a_weights: bfloat16 [4, 4096, 2048], P('rep', 'row', 'col'), may hold values from 0 to 10000, as said below
- a_flags: int32 [4, 32, 16], P('rep', 'row', 'col'), may hold values 0 or 1
- b_weights: bfloat16 [4, 2048, 32768], P('rep', 'row', 'col'), may hold values from 0 to 10000, as said below
- b_flags: int32 [4, 16, 256], P('rep', 'row', 'col'), may hold values 0 or 1
- out_flags: int32 [32, 256], P('row', ('col', 'rep')), may hold values 0 or 1
Outputs:
- two_hop: bfloat16 [4096, 32768], P('row', ('col', 'rep'))
The draws below stay inside these ranges and needn't reach their ends.
Inputs may be any that keep to these rules, and one draw needn't show every extreme that they name: `a_weights`: positive edge weights. `b_weights`: positive edge weights.
All inputs are finite; a program needn't handle non-finite values. No bound on the sum of `a_flags` or of `b_flags` or of `out_flags` on one device may be relied on, other than what follows from the above.
Results may differ from the reference program's by a relative error of at most 0.012.
Values may be sent and summed in bfloat16 or wider, within the bound.
No kernel may reach another device: no remote copies, remote signals or barrier semaphores. Data moves between devices by JAX's collectives and lax.ppermute only.
A program may use at most 64 MiB of HBM per device.

```python
import math
import jax
import jax.numpy as jnp
from jax import lax

TILE = 128
MB = 32
KG = 4
KW = 16
NB = 256


def heavy_weights(key, groups, rows, cols):
    first, second, third = jax.random.split(key, 3)
    normal_part = jnp.clip(jax.random.normal(first, (groups, rows, cols), jnp.float32), -3.5, 3.5)
    base = jnp.exp(1.2 * normal_part)
    col_scale = jnp.exp(math.log(10.0) * jax.random.uniform(second, (groups, 1, cols), jnp.float32))
    row_scale = jnp.exp(math.log(4.0) * jax.random.uniform(third, (groups, rows, 1), jnp.float32))
    ramp = 1.0 + 2.0 * jnp.arange(cols, dtype=jnp.float32) / cols
    return (base * col_scale * row_scale * ramp[None, None, :]).astype(jnp.bfloat16)


def draw_a_weights(key, part):
    return heavy_weights(jax.random.fold_in(key, 11), KG, MB * TILE, KW * TILE)


def draw_b_weights(key, part):
    return heavy_weights(jax.random.fold_in(key, 23), KG, KW * TILE, NB * TILE)


def with_ends(entries, stream_key, low, top_value):
    extent = entries.shape
    spot = [jax.random.randint(jax.random.fold_in(stream_key, axis), (), 0, extent[axis]) for axis in range(len(extent))]
    entries = entries.at[tuple(spot)].set(low)
    longest = extent.index(max(extent))
    spot[longest] = (spot[longest] + 1) % extent[longest]
    return entries.at[tuple(spot)].set(top_value)


def setup_inputs(seed: int = 0) -> dict:
    key_of = jax.random.split(jax.random.key(seed), 6)
    a_weights = draw_a_weights(jax.random.fold_in(key_of[5], 71), 0)
    a_flags = with_ends((jax.random.randint(key_of[1], (KG, MB, KW), 0, 2) < 1).astype(jnp.int32), jax.random.fold_in(key_of[1], 1), 0, 1)
    b_weights = draw_b_weights(jax.random.fold_in(key_of[5], 71), 0)
    b_flags = with_ends((jax.random.randint(key_of[3], (KG, KW, NB), 0, 2) < 1).astype(jnp.int32), jax.random.fold_in(key_of[3], 1), 0, 1)
    out_flags = with_ends((jax.random.randint(key_of[4], (MB, NB), 0, 3) < 2).astype(jnp.int32), jax.random.fold_in(key_of[4], 1), 0, 1)
    return dict(a_weights=a_weights, a_flags=a_flags, b_weights=b_weights, b_flags=b_flags, out_flags=out_flags)


def expand(flags):
    return jnp.repeat(jnp.repeat(flags, TILE, axis=-2), TILE, axis=-1)


def reference(a_weights, a_flags, b_weights, b_flags, out_flags):
    a_masked = a_weights * expand(a_flags).astype(jnp.bfloat16)
    deg_a = 1.0 + jnp.sum(a_masked.astype(jnp.float32), axis=(0, 2))
    walk_a = (a_masked.astype(jnp.float32) / deg_a[None, :, None]).astype(jnp.bfloat16)
    total = jnp.zeros((MB * TILE, NB * TILE), jnp.float32)
    for group in range(KG):
        b_masked = b_weights[group] * expand(b_flags[group]).astype(jnp.bfloat16)
        deg_b = 1.0 + jnp.sum(b_masked.astype(jnp.float32), axis=1)
        walk_b = (b_masked.astype(jnp.float32) / deg_b[:, None]).astype(jnp.bfloat16)
        group_part = jnp.dot(walk_a[group], walk_b, preferred_element_type=jnp.float32).astype(jnp.bfloat16)
        group_part = lax.optimization_barrier(group_part)
        total = total + group_part.astype(jnp.float32)
    factor = jnp.float32(NB * TILE)
    return (factor * total * expand(out_flags).astype(jnp.float32)).astype(jnp.bfloat16)
```

```python
import functools

import jax
import jax.numpy as jnp
from jax import lax
from jax.experimental import pallas as pl
from jax.experimental.pallas import tpu as pltpu
from jax.sharding import PartitionSpec as P

TILE = 128
F32, BF16 = jnp.float32, jnp.bfloat16
TURN = (1, -1, 1, -1)
ROWS = {h: [(4 * y + r, 4 * ((y + h * TURN[r]) % 4) + r) for y in range(4) for r in range(4)] for h in (1, 2, 3)}
ALONG_X = [
    (16 * x + 4 * z + r, 16 * ((x + TURN[r]) % 4) + 4 * z + r)
    for x in range(4) for z in range(4) for r in range(4)
]
ALONG_Z = [
    (16 * x + 4 * z + r, 16 * x + 4 * ((z + TURN[r]) % 4) + r)
    for x in range(4) for z in range(4) for r in range(4)
]
SWAP = {k: [(i, i ^ k) for i in range(4)] for k in (1, 2)}
COLS = {k: [(i, i ^ k) for i in range(16)] for k in (1, 2, 4, 8)}


def prep_kernel(rep_ref, flags_ref, b_ref, o_ref, *, chunk):
    p = pl.program_id(0)
    q = (p >> 1) | ((p & 1) << 1)
    column = (rep_ref[0] ^ q) * 4 + chunk
    for k in range(4):
        rows = pl.ds(TILE * k, TILE)
        on = flags_ref[k, column] != 0
        o_ref[rows, :] = jnp.where(on, b_ref[rows, :], jnp.zeros((TILE, TILE), BF16))


def prep(rep, flags, b, chunk):
    def source(p, rep_ref, flags_ref):
        q = (p >> 1) | ((p & 1) << 1)
        return 0, (rep_ref[0] ^ q) * 4 + chunk

    return pl.pallas_call(
        functools.partial(prep_kernel, chunk=chunk),
        grid_spec=pltpu.PrefetchScalarGridSpec(
            num_scalar_prefetch=2,
            grid=(4,),
            in_specs=[pl.BlockSpec((512, TILE), source)],
            out_specs=pl.BlockSpec((512, TILE), lambda p, rep_ref, flags_ref: (0, p)),
        ),
        out_shape=jax.ShapeDtypeStruct((512, 512), BF16),
        cost_estimate=pl.CostEstimate(flops=0, bytes_accessed=1 << 20, transcendentals=0),
    )(rep, flags, b)


def assemble_kernel(place_ref, scale_ref, *refs):
    pieces, o_ref = refs[:8], refs[8]
    for g in range(4):
        t = (g - place_ref[0]) & 3
        for j in range(4):
            z = (place_ref[1] - j * place_ref[2]) & 3
            piece = pieces[2 * g + j // 2][:, TILE * (j % 2):TILE * (j % 2 + 1)]
            scale = scale_ref[t, pl.ds(z, 1), :]
            o_ref[t, z] = (piece.astype(F32) * scale).astype(BF16)


def assemble(place, scale, pieces):
    return pl.pallas_call(
        assemble_kernel,
        grid_spec=pltpu.PrefetchScalarGridSpec(
            num_scalar_prefetch=1,
            grid=(4,),
            in_specs=[pl.BlockSpec((4, 4, TILE), lambda i, t: (0, 0, 0))]
            + [pl.BlockSpec((256, 256), lambda i, t: (i, 0))] * 8,
            out_specs=pl.BlockSpec((4, 4, 256, TILE), lambda i, t: (0, 0, i, 0)),
        ),
        out_shape=jax.ShapeDtypeStruct((4, 4, 1024, TILE), BF16),
        cost_estimate=pl.CostEstimate(flops=1 << 21, bytes_accessed=8 << 20, transcendentals=0),
    )(place, scale, *pieces)


def product_kernel(a_ref, *refs):
    hops, (k0_ref, k2_ref, s_ref) = refs[:4], refs[4:]
    total = jnp.zeros((256, 512), F32)
    for h in range(4):
        left = jnp.concatenate([a_ref[h, z] for z in range(4)], 1)
        total += jnp.dot(left, hops[h][...], preferred_element_type=F32)
    k0_ref[...] = total[:, :128]
    k2_ref[...] = total[:, 128:256]
    s_ref[...] = total[:, 256:].astype(BF16)


def product(a, hops):
    return pl.pallas_call(
        product_kernel,
        grid=(4,),
        in_specs=[pl.BlockSpec((4, 4, 256, TILE), lambda i: (0, 0, i, 0))]
        + [pl.BlockSpec((512, 512), lambda i: (0, 0))] * 4,
        out_specs=[
            pl.BlockSpec((256, 128), lambda i: (i, 0)),
            pl.BlockSpec((256, 128), lambda i: (i, 0)),
            pl.BlockSpec((256, 256), lambda i: (i, 0)),
        ],
        out_shape=[
            jax.ShapeDtypeStruct((1024, 128), F32),
            jax.ShapeDtypeStruct((1024, 128), F32),
            jax.ShapeDtypeStruct((1024, 256), BF16),
        ],
        compiler_params=pltpu.CompilerParams(vmem_limit_bytes=32 << 20),
        cost_estimate=pl.CostEstimate(flops=2 * 1024 * 2048 * 512, bytes_accessed=8 << 20, transcendentals=0),
    )(a, *hops)


def after(value, *others):
    return lax.optimization_barrier((value, *others))[0]


def shards(a_weights, a_flags, b_weights, b_flags, out_flags):
    rep = lax.axis_index("rep").astype(jnp.int32)
    row = lax.axis_index("row").astype(jnp.int32)
    col = lax.axis_index("col").astype(jnp.int32)
    x, z, turn = col >> 2, col & 3, 1 - 2 * (rep & 1)
    b, bf = b_weights[0], b_flags[0]
    chunks = [prep(rep[None], bf, b, c) for c in range(4)]
    a = a_weights[0] * jnp.repeat(a_flags[0, :, 0], TILE).astype(BF16)[:, None]

    hops = [[v] for v in chunks]
    for c in range(4):
        if c >= 2:
            hops[c][0] = after(hops[c][0], hops[c - 2][3])
        for h in range(3):
            hops[c].append(lax.ppermute(hops[c][h], ("row", "rep"), ROWS[1]))
        hops[c][0] = chunks[c]

    along_z = [a]
    for h in range(3):
        along_z.append(lax.ppermute(along_z[h], ("col", "rep"), ALONG_Z))
    near = [jnp.concatenate(along_z[:2], 1)]
    far = [jnp.concatenate(along_z[2:], 1)]
    for h in range(3):
        near.append(lax.ppermute(near[h], ("col", "rep"), ALONG_X))
        far.append(lax.ppermute(far[h], ("col", "rep"), ALONG_X))
    pieces = [v for pair in zip(near, far) for v in pair]

    a_sum = jnp.sum(a, axis=1, dtype=F32)
    b_sum = sum(jnp.sum(v, axis=1, dtype=F32) for v in chunks)
    sums = jnp.concatenate([a_sum, b_sum])
    for k in (1, 2, 4, 8):
        sums = sums + lax.ppermute(sums, "col", COLS[k])
    walk_b = 1.0 / (1.0 + sums[1024:])
    scale = jnp.stack([walk_b] + [lax.ppermute(walk_b, ("row", "rep"), ROWS[h]) for h in (1, 2, 3)], 0)
    deg_a = sums[:1024]
    for k in (1, 2):
        deg_a = deg_a + lax.ppermute(deg_a, "rep", SWAP[k])
    row_scale = (jnp.float32(TILE * 256) / (1.0 + deg_a))[:, None]

    place = jnp.stack([(x - row) * turn, z, turn])
    full = assemble(place, scale.reshape(4, 4, TILE), pieces)

    done = []
    for c in range(4):
        k0, k2, send = product(full, hops[c])
        got = lax.ppermute(send, "rep", SWAP[1])
        onward = (k2 + got[:, 128:].astype(F32)).astype(BF16)
        last = lax.ppermute(onward, "rep", SWAP[2])
        total = k0 + got[:, :128].astype(F32) + last.astype(F32)
        on = jnp.repeat(out_flags[:, c], TILE).astype(F32)[:, None]
        done.append((row_scale * total * on).astype(BF16))
    return jnp.concatenate(done, 1)


def solution(mesh):
    return jax.shard_map(
        shards,
        mesh=mesh,
        in_specs=(
            P("rep", "row", "col"),
            P("rep", "row", "col"),
            P("rep", "row", "col"),
            P("rep", "row", "col"),
            P("row", ("col", "rep")),
        ),
        out_specs=P("row", ("col", "rep")),
        check_vma=False,
    )
```

```python
import functools

import jax
import jax.numpy as jnp
from jax import lax
from jax.experimental import pallas as pl
from jax.experimental.pallas import tpu as pltpu
from jax.sharding import PartitionSpec as P

TILE = 128
F32, BF16 = jnp.float32, jnp.bfloat16
TURN = (1, -1, 1, -1)
ALONG_Y = {
    h: [(4 * y + r, 4 * ((y + h * TURN[r]) % 4) + r) for y in range(4) for r in range(4)] for h in (1, 2, 3)
}
ALONG_X = {s: [(4 * x + z, 4 * ((x + s) % 4) + z) for x in range(4) for z in range(4)] for s in (1, 3)}
ALONG_Z = {s: [(4 * x + z, 4 * x + (z + s) % 4) for x in range(4) for z in range(4)] for s in (1, 3)}
SWAP = {k: [(i, i ^ k) for i in range(4)] for k in (1, 2)}
COLS = {k: [(i, i ^ k) for i in range(16)] for k in (1, 2, 4, 8)}
VMEM = 14 << 20
TINY = pl.CostEstimate(flops=1, bytes_accessed=1, transcendentals=0)


def prep_kernel(place_ref, flags_ref, b_ref, o_ref, sum_ref, *, first):
    ones = jnp.ones((8, 512), BF16)
    block = place_ref[3] ^ (first - pl.program_id(0))
    for j in range(4):
        z = (place_ref[2] - j) & 3
        rows = pl.ds(pl.multiple_of(z * TILE, TILE), TILE)
        tiles = []
        for p in range(4):
            on = flags_ref[z, block * 4 + p] != 0
            tiles.append(jnp.where(on, b_ref[rows, TILE * p:TILE * (p + 1)], jnp.zeros((TILE, TILE), BF16)))
        line = jnp.concatenate(tiles, 1)
        o_ref[TILE * j:TILE * (j + 1), :] = line
        sum_ref[0, z] = lax.dot_general(ones, line, (((1,), (1,)), ((), ())), preferred_element_type=F32)


def prep(place, flags, b, first):
    return pl.pallas_call(
        functools.partial(prep_kernel, first=first),
        grid_spec=pltpu.PrefetchScalarGridSpec(
            num_scalar_prefetch=2,
            grid=(2,),
            in_specs=[pl.BlockSpec((512, 512), lambda i, place, flags: (0, place[3] ^ (first - i)))],
            out_specs=[
                pl.BlockSpec((512, 512), lambda i, place, flags: (0, i)),
                pl.BlockSpec((1, 4, 8, TILE), lambda i, place, flags: (i, 0, 0, 0)),
            ],
        ),
        out_shape=[jax.ShapeDtypeStruct((512, 1024), BF16), jax.ShapeDtypeStruct((2, 4, 8, TILE), F32)],
        compiler_params=pltpu.CompilerParams(vmem_limit_bytes=VMEM),
        cost_estimate=TINY,
    )(place, flags, b)


def mask_kernel(flags_ref, a_ref, o_ref):
    for k in range(8):
        rows = slice(TILE * k, TILE * (k + 1))
        o_ref[rows, :] = jnp.where(flags_ref[k] != 0, a_ref[rows, :], jnp.zeros((TILE, TILE), BF16))


def mask(flags, a):
    return pl.pallas_call(
        mask_kernel,
        grid_spec=pltpu.PrefetchScalarGridSpec(
            num_scalar_prefetch=1,
            grid=(1,),
            in_specs=[pl.BlockSpec((1024, TILE), lambda i, flags: (0, 0))],
            out_specs=pl.BlockSpec((1024, TILE), lambda i, flags: (0, 0)),
        ),
        out_shape=jax.ShapeDtypeStruct((1024, TILE), BF16),
        compiler_params=pltpu.CompilerParams(vmem_limit_bytes=VMEM),
        cost_estimate=TINY,
    )(flags, a)


def slot(place_ref, s):
    return ((place_ref[1] - place_ref[0] + s) * (1 - 2 * (place_ref[3] & 1))) & 3


def scaled(place_ref, scale_ref, piece, s):
    z = place_ref[2]
    scale = [scale_ref[slot(place_ref, s), pl.ds((z - j) & 3, 1), :] for j in range(4)]
    return (piece.astype(F32) * jnp.concatenate(scale, 1)).astype(BF16)


def row_sums(piece):
    ones = jnp.ones((8, 512), BF16)
    return lax.dot_general(ones, piece, (((1,), (1,)), ((), ())), preferred_element_type=F32)


def early_kernel(place_ref, scale_ref, own_ref, r_ref, l_ref, o_ref, sum_ref):
    total = jnp.zeros((8, 256), F32)
    for s, ref in ((0, own_ref), (1, r_ref), (3, l_ref)):
        o_ref[slot(place_ref, s)] = scaled(place_ref, scale_ref, ref[...], s)
        total += row_sums(ref[...])
    sum_ref[0] = total


SCALE = pl.BlockSpec((4, 4, TILE), lambda i, *_: (0, 0, 0))
SUMS = pl.BlockSpec((1, 8, 256), lambda i, *_: (i, 0, 0))
ROWS = pl.BlockSpec((256, 512), lambda i, *_: (i, 0))
ALL = pl.BlockSpec((4, 256, 512), lambda i, *_: (0, i, 0))
UPPER = pl.BlockSpec((256, 512), lambda i, *_: (jnp.minimum(i, 1), 0))
LOWER = pl.BlockSpec((256, 512), lambda i, *_: (jnp.maximum(i - 2, 0), 0))


def early(place, scale, pieces):
    return pl.pallas_call(
        early_kernel,
        grid_spec=pltpu.PrefetchScalarGridSpec(
            num_scalar_prefetch=1,
            grid=(4,),
            in_specs=[SCALE, ROWS, ROWS, ROWS],
            out_specs=[ALL, SUMS],
        ),
        out_shape=[jax.ShapeDtypeStruct((4, 1024, 512), BF16), jax.ShapeDtypeStruct((4, 8, 256), F32)],
        compiler_params=pltpu.CompilerParams(vmem_limit_bytes=VMEM),
        cost_estimate=TINY,
    )(place, scale, *pieces)


def multiply(a_ref, hops):
    total = jnp.dot(a_ref[0], hops[0][...], preferred_element_type=F32)
    for h in range(1, 4):
        total += jnp.dot(a_ref[h], hops[h][...], preferred_element_type=F32)
    return total


def hop_specs(q):
    return [pl.BlockSpec((512, 512), lambda i, *_: (0, q))] * 4


def opening_kernel(place_ref, scale_ref, full_ref, sums_ref, r2_ref, l2_ref, *refs):
    hops, (last_ref, o_ref, total_ref) = refs[:4], refs[4:]
    piece = jnp.where(pl.program_id(0) < 2, r2_ref[...], l2_ref[...])
    last = scaled(place_ref, scale_ref, piece, 2)
    last_ref[0] = last
    total_ref[0] = sums_ref[0] + row_sums(piece)
    missing = slot(place_ref, 2)
    lefts = [jnp.where(missing == h, last, full_ref[h]) for h in range(4)]
    o_ref[...] = multiply(lefts, hops).astype(BF16)


def opening(place, scale, full, sums, r2, l2, hops, q):
    return pl.pallas_call(
        opening_kernel,
        grid_spec=pltpu.PrefetchScalarGridSpec(
            num_scalar_prefetch=1,
            grid=(4,),
            in_specs=[SCALE, ALL, SUMS, UPPER, LOWER] + hop_specs(q),
            out_specs=[
                pl.BlockSpec((1, 256, 512), lambda i, place: (slot(place, 2), i, 0)),
                ROWS,
                SUMS,
            ],
        ),
        out_shape=[
            jax.ShapeDtypeStruct((4, 1024, 512), BF16),
            jax.ShapeDtypeStruct((1024, 512), BF16),
            jax.ShapeDtypeStruct((4, 8, 256), F32),
        ],
        input_output_aliases={2: 0},
        compiler_params=pltpu.CompilerParams(vmem_limit_bytes=VMEM),
        cost_estimate=TINY,
    )(place, scale, full, sums, r2, l2, *hops)


def product_kernel(a_ref, *refs):
    refs[4][...] = multiply(a_ref, refs[:4]).astype(refs[4].dtype)


def product(a, hops, q, dtype, start=0, steps=4):
    return pl.pallas_call(
        product_kernel,
        grid=(steps,),
        in_specs=[pl.BlockSpec((4, 256, 512), lambda i: (0, start + i, 0))] + hop_specs(q),
        out_specs=ROWS,
        out_shape=jax.ShapeDtypeStruct((256 * steps, 512), dtype),
        compiler_params=pltpu.CompilerParams(vmem_limit_bytes=VMEM),
        cost_estimate=TINY,
    )(a, *hops)


def closing_kernel(flags_ref, part_ref, upper_ref, lower_ref, chip_ref, sum_ref, more_ref, o_ref):
    core = jnp.where(pl.program_id(0) < 2, upper_ref[...], lower_ref[...])
    total = part_ref[...] + core.astype(F32)
    total += chip_ref[...].astype(F32)
    scale = jnp.float32(TILE * 256) / (1.0 + sum_ref[0] + more_ref[0])
    total *= jnp.transpose(scale)[:, 0:1]
    for k in range(2):
        rows = slice(TILE * k, TILE * (k + 1))
        for p in range(4):
            lanes = slice(TILE * p, TILE * (p + 1))
            on = flags_ref[2 * pl.program_id(0) + k, p] != 0
            o_ref[rows, lanes] = jnp.where(on, total[rows, lanes], 0.0).astype(BF16)


def closing(flags, part, upper, lower, chip, sums, more):
    return pl.pallas_call(
        closing_kernel,
        grid_spec=pltpu.PrefetchScalarGridSpec(
            num_scalar_prefetch=1,
            grid=(4,),
            in_specs=[ROWS, UPPER, LOWER, ROWS, SUMS, SUMS],
            out_specs=ROWS,
        ),
        out_shape=jax.ShapeDtypeStruct((1024, 512), BF16),
        compiler_params=pltpu.CompilerParams(vmem_limit_bytes=VMEM),
        cost_estimate=TINY,
    )(flags, part, upper, lower, chip, sums, more)


class Order:
    def __init__(self):
        self.seen = []

    def send(self, value, axes, pairs):
        others = [v for v in self.seen[-5:] if v is not value]
        if others:
            value = lax.optimization_barrier((value, *others))[0]
        return lax.ppermute(value, axes, pairs)

    def wait(self, *values):
        self.seen.extend(values)


def shards(a_weights, a_flags, b_weights, b_flags, out_flags):
    rep = lax.axis_index("rep").astype(jnp.int32)
    row = lax.axis_index("row").astype(jnp.int32)
    col = lax.axis_index("col").astype(jnp.int32)
    place = jnp.stack([col >> 2, row, col & 3, rep])
    b, bf = b_weights[0], b_flags[0]
    order = Order()

    def both(v, axis, tables):
        return order.send(v, axis, tables[1]), order.send(v, axis, tables[3])

    def onward(r, l, axis, tables):
        n = r.shape[0] // 2
        return order.send(r[:n], axis, tables[1]), order.send(l[n:], axis, tables[3])

    def send_y(v, h=1):
        return order.send(v, ("row", "rep"), ALONG_Y[h])

    a = mask(a_flags[0, :, 0], a_weights[0])
    zr, zl = both(a, "col", ALONG_Z)
    b, a = lax.optimization_barrier((b, a))
    b32, sum32 = prep(place, bf, b, 3)
    h32 = [b32, send_y(b32)]
    b10, sum10 = prep(place, bf, lax.optimization_barrier((b, sum32))[0], 1)
    h10 = [b10, send_y(b10)]
    total = (sum32[0] + sum32[1] + sum10[0] + sum10[1])[:, 0, :]
    other = order.send(total, "col", COLS[4])
    order.wait(other)
    total = total + other
    other = order.send(total, "col", COLS[8])
    order.wait(other, zr, zl)
    total = total + other
    zr2, zl2 = onward(zr, zl, "col", ALONG_Z)
    order.wait(h32[1])
    h32.append(send_y(h32[1]))
    order.wait(zr2, zl2)
    wide = jnp.concatenate([a, zr, jnp.concatenate([zr2, zl2], 0), zl], 1)
    xr, xl = both(wide, "col", ALONG_X)
    other = order.send(total, "col", COLS[1])
    order.wait(other)
    total = total + other
    other = order.send(total, "col", COLS[2])
    order.wait(other, h10[1])
    total = total + other
    walk_b = 1.0 / (1.0 + total)
    others = [send_y(walk_b, h) for h in (1, 2, 3)]
    order.wait(h32[2], *others)
    scale = jnp.stack([walk_b] + others, 0)
    h32.append(send_y(h32[2]))

    order.wait(xr, xl)
    xr2, xl2 = onward(xr, xl, "col", ALONG_X)
    h10.append(send_y(h10[1]))
    most, some = early(place, scale, (wide, xr, xl))
    full, part3, sums = opening(place, scale, most, some, xr2, xl2, h32, 0)
    order.wait(part3)
    core3 = order.send(part3, "rep", SWAP[1])
    more = order.send(sums, "rep", SWAP[1])
    order.wait(h10[2])
    part2 = product(full, [lax.optimization_barrier((h32[0], h10[2]))[0]] + h32[1:], 1, F32)
    order.wait(more, part2)
    sums = sums + more
    more = order.send(sums, "rep", SWAP[2])
    pair = (part2 + core3.astype(F32)).astype(BF16)
    chip = order.send(pair, "rep", SWAP[2])
    h10.append(send_y(h10[2]))
    h10[3] = lax.optimization_barrier((h10[3], pair))[0]
    part1 = product(full, h10, 0, BF16, 0, 2), product(full, h10, 0, BF16, 2, 2)
    part0 = product(full, h10, 1, F32)
    order.wait(part0)
    upper, lower = (order.send(v, "rep", SWAP[1]) for v in part1)
    return closing(out_flags, part0, upper, lower, chip, sums, more)


def solution(mesh):
    return jax.shard_map(
        shards,
        mesh=mesh,
        in_specs=(
            P("rep", "row", "col"),
            P("rep", "row", "col"),
            P("rep", "row", "col"),
            P("rep", "row", "col"),
            P("row", ("col", "rep")),
        ),
        out_specs=P("row", ("col", "rep")),
        check_vma=False,
    )
```

```python
import functools

import jax
import jax.numpy as jnp
from jax import lax
from jax.experimental import pallas as pl
from jax.experimental.pallas import tpu as pltpu
from jax.sharding import PartitionSpec as P

TILE = 128
F32, BF16 = jnp.float32, jnp.bfloat16
TURN = (1, -1, 1, -1)
ALONG_Y = {
    h: [(4 * y + r, 4 * ((y + h * TURN[r]) % 4) + r) for y in range(4) for r in range(4)] for h in (1, 2, 3)
}
ALONG_X = {s: [(4 * x + z, 4 * ((x + s) % 4) + z) for x in range(4) for z in range(4)] for s in (1, 3)}
ALONG_Z = {s: [(4 * x + z, 4 * x + (z + s) % 4) for x in range(4) for z in range(4)] for s in (1, 3)}
SWAP = {k: [(i, i ^ k) for i in range(4)] for k in (1, 2)}
COLS = {k: [(i, i ^ k) for i in range(16)] for k in (1, 2, 4, 8)}
VMEM = 14 << 20
WAIT = 160 << 20
PAUSE = 8 << 20
TINY = pl.CostEstimate(flops=1, bytes_accessed=1, transcendentals=0)


def prep_kernel(place_ref, flags_ref, b_ref, o_ref, sum_ref, *, first):
    ones = jnp.ones((8, 512), BF16)
    block = place_ref[3] ^ (first - pl.program_id(0))
    for j in range(4):
        z = (place_ref[2] - j) & 3
        rows = pl.ds(pl.multiple_of(z * TILE, TILE), TILE)
        tiles = []
        for p in range(4):
            on = flags_ref[z, block * 4 + p] != 0
            tiles.append(jnp.where(on, b_ref[rows, TILE * p:TILE * (p + 1)], jnp.zeros((TILE, TILE), BF16)))
        line = jnp.concatenate(tiles, 1)
        o_ref[TILE * j:TILE * (j + 1), :] = line
        sum_ref[0, z] = lax.dot_general(ones, line, (((1,), (1,)), ((), ())), preferred_element_type=F32)


def prep(place, flags, b, first):
    return pl.pallas_call(
        functools.partial(prep_kernel, first=first),
        grid_spec=pltpu.PrefetchScalarGridSpec(
            num_scalar_prefetch=2,
            grid=(2,),
            in_specs=[pl.BlockSpec((512, 512), lambda i, place, flags: (0, place[3] ^ (first - i)))],
            out_specs=[
                pl.BlockSpec((512, 512), lambda i, place, flags: (0, i)),
                pl.BlockSpec((1, 4, 8, TILE), lambda i, place, flags: (i, 0, 0, 0)),
            ],
        ),
        out_shape=[jax.ShapeDtypeStruct((512, 1024), BF16), jax.ShapeDtypeStruct((2, 4, 8, TILE), F32)],
        compiler_params=pltpu.CompilerParams(vmem_limit_bytes=VMEM),
        cost_estimate=TINY,
    )(place, flags, b)


def mask_kernel(flags_ref, a_ref, o_ref, sum_ref):
    ones = jnp.ones((8, TILE), BF16)
    for k in range(8):
        rows = slice(TILE * k, TILE * (k + 1))
        tile = jnp.where(flags_ref[k] != 0, a_ref[rows, :], jnp.zeros((TILE, TILE), BF16))
        o_ref[rows, :] = tile
        sum_ref[k] = lax.dot_general(ones, tile, (((1,), (1,)), ((), ())), preferred_element_type=F32)


def mask(flags, a):
    return pl.pallas_call(
        mask_kernel,
        grid_spec=pltpu.PrefetchScalarGridSpec(
            num_scalar_prefetch=1,
            grid=(1,),
            in_specs=[pl.BlockSpec((1024, TILE), lambda i, flags: (0, 0))],
            out_specs=[
                pl.BlockSpec((1024, TILE), lambda i, flags: (0, 0)),
                pl.BlockSpec((8, 8, TILE), lambda i, flags: (0, 0, 0)),
            ],
        ),
        out_shape=[jax.ShapeDtypeStruct((1024, TILE), BF16), jax.ShapeDtypeStruct((8, 8, TILE), F32)],
        compiler_params=pltpu.CompilerParams(vmem_limit_bytes=VMEM),
        cost_estimate=TINY,
    )(flags, a)


def gather_kernel(own_ref, r_ref, l_ref, r2_ref, l2_ref, o_ref):
    o_ref[:, :TILE] = own_ref[...]
    o_ref[:, TILE:2 * TILE] = r_ref[...]
    o_ref[:512, 2 * TILE:3 * TILE] = r2_ref[...]
    o_ref[512:, 2 * TILE:3 * TILE] = l2_ref[...]
    o_ref[:, 3 * TILE:] = l_ref[...]


def gather(own, r, l, r2, l2):
    return pl.pallas_call(
        gather_kernel,
        out_shape=jax.ShapeDtypeStruct((1024, 512), BF16),
        compiler_params=pltpu.CompilerParams(vmem_limit_bytes=VMEM),
        cost_estimate=pl.CostEstimate(flops=1, bytes_accessed=WAIT, transcendentals=0),
    )(own, r, l, r2, l2)


def slot(place_ref, s):
    return ((place_ref[1] - place_ref[0] + s) * (1 - 2 * (place_ref[3] & 1))) & 3


def scaled(place_ref, scale_ref, piece, s):
    z = place_ref[2]
    scale = [scale_ref[slot(place_ref, s), pl.ds((z - j) & 3, 1), :] for j in range(4)]
    return (piece.astype(F32) * jnp.concatenate(scale, 1)).astype(BF16)


def early_kernel(place_ref, scale_ref, own_ref, r_ref, l_ref, o_ref):
    for s, ref in ((0, own_ref), (1, r_ref), (3, l_ref)):
        o_ref[slot(place_ref, s)] = scaled(place_ref, scale_ref, ref[...], s)


SCALE = pl.BlockSpec((4, 4, TILE), lambda i, *_: (0, 0, 0))
ROWS = pl.BlockSpec((256, 512), lambda i, *_: (i, 0))
ALL = pl.BlockSpec((4, 256, 512), lambda i, *_: (0, i, 0))
UPPER = pl.BlockSpec((256, 512), lambda i, *_: (jnp.minimum(i, 1), 0))
LOWER = pl.BlockSpec((256, 512), lambda i, *_: (jnp.maximum(i - 2, 0), 0))


def early(place, scale, pieces):
    return pl.pallas_call(
        early_kernel,
        grid_spec=pltpu.PrefetchScalarGridSpec(
            num_scalar_prefetch=1,
            grid=(4,),
            in_specs=[SCALE, ROWS, ROWS, ROWS],
            out_specs=ALL,
        ),
        out_shape=jax.ShapeDtypeStruct((4, 1024, 512), BF16),
        compiler_params=pltpu.CompilerParams(vmem_limit_bytes=VMEM),
        cost_estimate=TINY,
    )(place, scale, *pieces)


def multiply(a_ref, hops):
    total = jnp.dot(a_ref[0], hops[0][...], preferred_element_type=F32)
    for h in range(1, 4):
        total += jnp.dot(a_ref[h], hops[h][...], preferred_element_type=F32)
    return total


def hop_specs(q):
    return [pl.BlockSpec((512, 512), lambda i, *_: (0, q))] * 4


def opening_kernel(place_ref, scale_ref, full_ref, piece_ref, *refs):
    hops, (last_ref, o_ref) = refs[:4], refs[4:]
    last = scaled(place_ref, scale_ref, piece_ref[...], 2)
    last_ref[0] = last
    missing = slot(place_ref, 2)
    lefts = [jnp.where(missing == h, last, full_ref[h]) for h in range(4)]
    o_ref[...] = multiply(lefts, hops).astype(BF16)


def opening(place, scale, full, piece, hops, half):
    return pl.pallas_call(
        opening_kernel,
        grid_spec=pltpu.PrefetchScalarGridSpec(
            num_scalar_prefetch=1,
            grid=(2,),
            in_specs=[SCALE, pl.BlockSpec((4, 256, 512), lambda i, *_: (0, 2 * half + i, 0)), ROWS] + hop_specs(0),
            out_specs=[
                pl.BlockSpec((1, 256, 512), lambda i, place: (slot(place, 2), 2 * half + i, 0)),
                ROWS,
            ],
        ),
        out_shape=[
            jax.ShapeDtypeStruct((4, 1024, 512), BF16),
            jax.ShapeDtypeStruct((512, 512), BF16),
        ],
        input_output_aliases={2: 0},
        compiler_params=pltpu.CompilerParams(vmem_limit_bytes=VMEM),
        cost_estimate=TINY,
    )(place, scale, full, piece, *hops)


def middle_kernel(full_ref, core_ref, *refs):
    refs[4][...] = (multiply(full_ref, refs[:4]) + core_ref[...].astype(F32)).astype(BF16)


def middle(full, core, hops, half):
    return pl.pallas_call(
        middle_kernel,
        grid=(2,),
        in_specs=[pl.BlockSpec((4, 256, 512), lambda i: (0, 2 * half + i, 0)), ROWS] + hop_specs(1),
        out_specs=ROWS,
        out_shape=jax.ShapeDtypeStruct((512, 512), BF16),
        compiler_params=pltpu.CompilerParams(vmem_limit_bytes=VMEM),
        cost_estimate=TINY,
    )(full, core, *hops)


def multiply_split(full_ref, hops):
    total = jnp.dot(full_ref[0], hops[0][...], preferred_element_type=F32)
    for h in range(1, 3):
        total += jnp.dot(full_ref[h], hops[h][...], preferred_element_type=F32)
    total += jnp.dot(full_ref[3, :, :256], hops[3][...], preferred_element_type=F32)
    return total + jnp.dot(full_ref[3, :, 256:], hops[4][...], preferred_element_type=F32)


def split_specs(q):
    return [pl.BlockSpec((512, 512), lambda i, *_: (0, q))] * 3 + [pl.BlockSpec((256, 512), lambda i, *_: (0, q))] * 2


def pieces_kernel(full_ref, *refs):
    total = multiply_split(full_ref, refs[:5]).astype(BF16)
    for k in range(2):

        @pl.when((pl.program_id(0) >> 1) == k)
        def _():
            refs[5 + k][...] = total


def pieces(full, hops):
    return pl.pallas_call(
        pieces_kernel,
        grid=(4,),
        in_specs=[ALL] + split_specs(0),
        out_specs=[UPPER, LOWER],
        out_shape=[jax.ShapeDtypeStruct((512, 512), BF16)] * 2,
        compiler_params=pltpu.CompilerParams(vmem_limit_bytes=VMEM),
        cost_estimate=TINY,
    )(full, *hops)


def product_kernel(full_ref, *refs):
    refs[5][...] = multiply_split(full_ref, refs[:5])


def product(full, hops):
    return pl.pallas_call(
        product_kernel,
        grid=(4,),
        in_specs=[ALL] + split_specs(1),
        out_specs=ROWS,
        out_shape=jax.ShapeDtypeStruct((1024, 512), F32),
        compiler_params=pltpu.CompilerParams(vmem_limit_bytes=VMEM),
        cost_estimate=TINY,
    )(full, *hops)


def closing_kernel(flags_ref, part_ref, core0_ref, core1_ref, chip0_ref, chip1_ref, sum_ref, more_ref, o_ref):
    step = pl.program_id(0)
    core = jnp.where(step == 0, core0_ref[...], core1_ref[...])
    chip = jnp.where(step == 0, chip0_ref[...], chip1_ref[...])
    for block in range(4):
        rows = slice(TILE * block, TILE * (block + 1))
        total = part_ref[rows, :] + core[rows, :].astype(F32)
        total += chip[rows, :].astype(F32)
        line = pl.ds(4 * step + block, 1)
        scale = jnp.float32(TILE * 256) / (1.0 + sum_ref[line, :] + more_ref[line, :])
        total *= jnp.transpose(jnp.broadcast_to(scale, (8, TILE)))[:, 0:1]
        for p in range(4):
            lanes = slice(TILE * p, TILE * (p + 1))
            on = flags_ref[4 * step + block, p] != 0
            o_ref[rows, lanes] = jnp.where(on, total[:, lanes], 0.0).astype(BF16)


def closing(flags, part, core, chip, sums, more):
    rows = pl.BlockSpec((512, 512), lambda i, f: (i, 0))
    side = pl.BlockSpec((8, TILE), lambda i, f: (0, 0))
    whole = pl.BlockSpec((512, 512), lambda i, f: (0, 0))
    return pl.pallas_call(
        closing_kernel,
        grid_spec=pltpu.PrefetchScalarGridSpec(
            num_scalar_prefetch=1,
            grid=(2,),
            in_specs=[rows, whole, whole, whole, whole, side, side],
            out_specs=rows,
        ),
        out_shape=jax.ShapeDtypeStruct((1024, 512), BF16),
        compiler_params=pltpu.CompilerParams(vmem_limit_bytes=VMEM),
        cost_estimate=TINY,
    )(flags, part, *core, *chip, sums, more)


class Order:
    def __init__(self):
        self.seen = []

    def send(self, value, axes, pairs):
        others = [v for v in self.seen[-5:] if v is not value]
        if others:
            value = lax.optimization_barrier((value, *others))[0]
        return lax.ppermute(value, axes, pairs)

    def wait(self, *values):
        self.seen.extend(values)


def shards(a_weights, a_flags, b_weights, b_flags, out_flags):
    rep = lax.axis_index("rep").astype(jnp.int32)
    row = lax.axis_index("row").astype(jnp.int32)
    col = lax.axis_index("col").astype(jnp.int32)
    place = jnp.stack([col >> 2, row, col & 3, rep])
    b, bf = b_weights[0], b_flags[0]
    order = Order()

    def both(v, axis, tables):
        return order.send(v, axis, tables[1]), order.send(v, axis, tables[3])

    def onward(r, l, axis, tables):
        n = r.shape[0] // 2
        return order.send(r[:n], axis, tables[1]), order.send(l[n:], axis, tables[3])

    def send_y(v, h=1):
        return order.send(v, ("row", "rep"), ALONG_Y[h])

    a, a_sum = mask(a_flags[0, :, 0], a_weights[0])
    zr, zl = both(a, "col", ALONG_Z)
    b, a = lax.optimization_barrier((b, a))
    b32, sum32 = prep(place, bf, b, 3)
    h32 = [b32, send_y(b32)]
    b10, sum10 = prep(place, bf, lax.optimization_barrier((b, sum32))[0], 1)
    h10 = [b10, send_y(b10)]
    b_sum = sum32[0] + sum32[1] + sum10[0] + sum10[1]
    total = jnp.concatenate([a_sum[:, 0, :], b_sum[:, 0, :]], 0)
    other = order.send(total, "col", COLS[4])
    order.wait(other)
    total = total + other
    other = order.send(total, "col", COLS[8])
    order.wait(other, zr, zl)
    total = total + other
    zr2, zl2 = onward(zr, zl, "col", ALONG_Z)
    order.wait(h32[1])
    h32.append(send_y(h32[1]))
    other = order.send(total, "col", COLS[1])
    wide = gather(a, zr, zl, zr2, zl2)
    order.wait(zr2, zl2, other)
    xr, xl = both(wide, "col", ALONG_X)
    total = total + other
    other = order.send(total, "col", COLS[2])
    h10.append(send_y(h10[1]))
    order.wait(h32[2], other)
    total = total + other
    walk_b = 1.0 / (1.0 + total[8:])
    others = [send_y(walk_b, h) for h in (1, 2, 3)]
    order.wait(h10[2], *others)
    scale = jnp.stack([walk_b] + others, 0)
    h32.append(send_y(h32[2]))

    order.wait(xr, xl)
    xr2, xl2 = onward(xr, xl, "col", ALONG_X)
    upper = send_y(h10[2][:256])
    sums = total[:8]
    more = order.send(sums, "rep", SWAP[1])
    most = early(place, scale, (wide, xr, xl))
    sums = sums + more
    more = order.send(sums, "rep", SWAP[2])
    xr2 = lax.optimization_barrier((xr2, more))[0]
    full, top3 = opening(place, scale, most, xr2, h32, 0)
    order.wait(top3)
    top_core = order.send(top3, "rep", SWAP[1])
    full, low3 = opening(place, scale, full, xl2, h32, 1)
    order.wait(low3)
    low_core = order.send(low3, "rep", SWAP[1])
    top2 = middle(full, top_core, h32, 0)
    order.wait(top2)
    top_chip = order.send(top2, "rep", SWAP[2])
    low2 = middle(full, low_core, [lax.optimization_barrier((h32[0], top2, upper))[0]] + h32[1:], 1)
    order.wait(low2)
    low_chip = order.send(low2, "rep", SWAP[2])
    lower = send_y(h10[2][256:])
    hops = h10 + [upper, lax.optimization_barrier((lower, low2))[0]]
    part1 = pieces(full, hops)
    part0 = product(full, hops)
    order.wait(part0)
    core = [order.send(v, "rep", SWAP[1]) for v in part1]
    return closing(out_flags, part0, core, (top_chip, low_chip), sums, more)


def solution(mesh):
    return jax.shard_map(
        shards,
        mesh=mesh,
        in_specs=(
            P("rep", "row", "col"),
            P("rep", "row", "col"),
            P("rep", "row", "col"),
            P("rep", "row", "col"),
            P("row", ("col", "rep")),
        ),
        out_specs=P("row", ("col", "rep")),
        check_vma=False,
    )
```

```python
import functools

import jax
import jax.numpy as jnp
from jax import lax
from jax.experimental import pallas as pl
from jax.experimental.pallas import tpu as pltpu
from jax.sharding import PartitionSpec as P

TILE = 128
F32, BF16 = jnp.float32, jnp.bfloat16
TURN = (1, -1, 1, -1)
ALONG_Y = {
    h: [(4 * y + r, 4 * ((y + h * TURN[r]) % 4) + r) for y in range(4) for r in range(4)] for h in (1, 2, 3)
}
ALONG_X = {s: [(4 * x + z, 4 * ((x + s) % 4) + z) for x in range(4) for z in range(4)] for s in (1, 3)}
ALONG_Z = {s: [(4 * x + z, 4 * x + (z + s) % 4) for x in range(4) for z in range(4)] for s in (1, 3)}
SWAP = {k: [(i, i ^ k) for i in range(4)] for k in (1, 2)}
COLS = {k: [(i, i ^ k) for i in range(16)] for k in (1, 2, 4, 8)}
VMEM = 14 << 20
WAIT = 160 << 20
PAUSE = 8 << 20
TINY = pl.CostEstimate(flops=1, bytes_accessed=1, transcendentals=0)


def prep_kernel(place_ref, flags_ref, b_ref, o_ref, sum_ref, *, first):
    ones = jnp.ones((8, 512), BF16)
    block = place_ref[3] ^ (first - pl.program_id(0))
    for j in range(4):
        z = (place_ref[2] - j) & 3
        rows = pl.ds(pl.multiple_of(z * TILE, TILE), TILE)
        tiles = []
        for p in range(4):
            on = flags_ref[z, block * 4 + p] != 0
            tiles.append(jnp.where(on, b_ref[rows, TILE * p:TILE * (p + 1)], jnp.zeros((TILE, TILE), BF16)))
        line = jnp.concatenate(tiles, 1)
        o_ref[TILE * j:TILE * (j + 1), :] = line
        sum_ref[0, z] = lax.dot_general(ones, line, (((1,), (1,)), ((), ())), preferred_element_type=F32)


def prep(place, flags, b, first):
    return pl.pallas_call(
        functools.partial(prep_kernel, first=first),
        grid_spec=pltpu.PrefetchScalarGridSpec(
            num_scalar_prefetch=2,
            grid=(2,),
            in_specs=[pl.BlockSpec((512, 512), lambda i, place, flags: (0, place[3] ^ (first - i)))],
            out_specs=[
                pl.BlockSpec((512, 512), lambda i, place, flags: (0, i)),
                pl.BlockSpec((1, 4, 8, TILE), lambda i, place, flags: (i, 0, 0, 0)),
            ],
        ),
        out_shape=[jax.ShapeDtypeStruct((512, 1024), BF16), jax.ShapeDtypeStruct((2, 4, 8, TILE), F32)],
        compiler_params=pltpu.CompilerParams(vmem_limit_bytes=VMEM),
        cost_estimate=TINY,
    )(place, flags, b)


def mask_kernel(flags_ref, a_ref, o_ref, sum_ref):
    ones = jnp.ones((8, TILE), BF16)
    for k in range(8):
        rows = slice(TILE * k, TILE * (k + 1))
        tile = jnp.where(flags_ref[k] != 0, a_ref[rows, :], jnp.zeros((TILE, TILE), BF16))
        o_ref[rows, :] = tile
        sum_ref[k] = lax.dot_general(ones, tile, (((1,), (1,)), ((), ())), preferred_element_type=F32)


def mask(flags, a):
    return pl.pallas_call(
        mask_kernel,
        grid_spec=pltpu.PrefetchScalarGridSpec(
            num_scalar_prefetch=1,
            grid=(1,),
            in_specs=[pl.BlockSpec((1024, TILE), lambda i, flags: (0, 0))],
            out_specs=[
                pl.BlockSpec((1024, TILE), lambda i, flags: (0, 0)),
                pl.BlockSpec((8, 8, TILE), lambda i, flags: (0, 0, 0)),
            ],
        ),
        out_shape=[jax.ShapeDtypeStruct((1024, TILE), BF16), jax.ShapeDtypeStruct((8, 8, TILE), F32)],
        compiler_params=pltpu.CompilerParams(vmem_limit_bytes=VMEM),
        cost_estimate=TINY,
    )(flags, a)


def gather_kernel(own_ref, r_ref, l_ref, r2_ref, l2_ref, o_ref):
    o_ref[:, :TILE] = own_ref[...]
    o_ref[:, TILE:2 * TILE] = r_ref[...]
    o_ref[:512, 2 * TILE:3 * TILE] = r2_ref[...]
    o_ref[512:, 2 * TILE:3 * TILE] = l2_ref[...]
    o_ref[:, 3 * TILE:] = l_ref[...]


def gather(own, r, l, r2, l2):
    return pl.pallas_call(
        gather_kernel,
        out_shape=jax.ShapeDtypeStruct((1024, 512), BF16),
        compiler_params=pltpu.CompilerParams(vmem_limit_bytes=VMEM),
        cost_estimate=pl.CostEstimate(flops=1, bytes_accessed=WAIT, transcendentals=0),
    )(own, r, l, r2, l2)


def slot(place_ref, s):
    return ((place_ref[1] - place_ref[0] + s) * (1 - 2 * (place_ref[3] & 1))) & 3


def scaled(place_ref, scale_ref, piece, s):
    z = place_ref[2]
    scale = [scale_ref[slot(place_ref, s), pl.ds((z - j) & 3, 1), :] for j in range(4)]
    return (piece.astype(F32) * jnp.concatenate(scale, 1)).astype(BF16)


def early_kernel(place_ref, scale_ref, own_ref, r_ref, l_ref, o_ref):
    for s, ref in ((0, own_ref), (1, r_ref), (3, l_ref)):
        o_ref[slot(place_ref, s)] = scaled(place_ref, scale_ref, ref[...], s)


SCALE = pl.BlockSpec((4, 4, TILE), lambda i, *_: (0, 0, 0))
ROWS = pl.BlockSpec((256, 512), lambda i, *_: (i, 0))
ALL = pl.BlockSpec((4, 256, 512), lambda i, *_: (0, i, 0))
UPPER = pl.BlockSpec((256, 512), lambda i, *_: (jnp.minimum(i, 1), 0))
LOWER = pl.BlockSpec((256, 512), lambda i, *_: (jnp.maximum(i - 2, 0), 0))


def early(place, scale, pieces):
    return pl.pallas_call(
        early_kernel,
        grid_spec=pltpu.PrefetchScalarGridSpec(
            num_scalar_prefetch=1,
            grid=(4,),
            in_specs=[SCALE, ROWS, ROWS, ROWS],
            out_specs=ALL,
        ),
        out_shape=jax.ShapeDtypeStruct((4, 1024, 512), BF16),
        compiler_params=pltpu.CompilerParams(vmem_limit_bytes=VMEM),
        cost_estimate=TINY,
    )(place, scale, *pieces)


def multiply(a_ref, hops):
    total = jnp.dot(a_ref[0], hops[0][...], preferred_element_type=F32)
    for h in range(1, 4):
        total += jnp.dot(a_ref[h], hops[h][...], preferred_element_type=F32)
    return total


def hop_specs(q):
    return [pl.BlockSpec((512, 512), lambda i, *_: (0, q))] * 4


def opening_kernel(place_ref, scale_ref, full_ref, piece_ref, *refs):
    hops, (last_ref, o_ref) = refs[:4], refs[4:]
    last = scaled(place_ref, scale_ref, piece_ref[...], 2)
    last_ref[0] = last
    missing = slot(place_ref, 2)
    lefts = [jnp.where(missing == h, last, full_ref[h]) for h in range(4)]
    o_ref[...] = multiply(lefts, hops).astype(BF16)


def opening(place, scale, full, piece, hops, half):
    return pl.pallas_call(
        opening_kernel,
        grid_spec=pltpu.PrefetchScalarGridSpec(
            num_scalar_prefetch=1,
            grid=(2,),
            in_specs=[SCALE, pl.BlockSpec((4, 256, 512), lambda i, *_: (0, 2 * half + i, 0)), ROWS] + hop_specs(0),
            out_specs=[
                pl.BlockSpec((1, 256, 512), lambda i, place: (slot(place, 2), 2 * half + i, 0)),
                ROWS,
            ],
        ),
        out_shape=[
            jax.ShapeDtypeStruct((4, 1024, 512), BF16),
            jax.ShapeDtypeStruct((512, 512), BF16),
        ],
        input_output_aliases={2: 0},
        compiler_params=pltpu.CompilerParams(vmem_limit_bytes=VMEM),
        cost_estimate=TINY,
    )(place, scale, full, piece, *hops)


def middle_kernel(full_ref, core_ref, *refs):
    refs[4][...] = (multiply(full_ref, refs[:4]) + core_ref[...].astype(F32)).astype(BF16)


def middle(full, core, hops, half):
    return pl.pallas_call(
        middle_kernel,
        grid=(2,),
        in_specs=[pl.BlockSpec((4, 256, 512), lambda i: (0, 2 * half + i, 0)), ROWS] + hop_specs(1),
        out_specs=ROWS,
        out_shape=jax.ShapeDtypeStruct((512, 512), BF16),
        compiler_params=pltpu.CompilerParams(vmem_limit_bytes=VMEM),
        cost_estimate=TINY,
    )(full, core, *hops)


def pieces_kernel(full_ref, *refs):
    total = multiply(full_ref, refs[:4]).astype(BF16)
    for k in range(2):

        @pl.when((pl.program_id(0) >> 1) == k)
        def _():
            refs[4 + k][...] = total


def pieces(full, hops):
    return pl.pallas_call(
        pieces_kernel,
        grid=(4,),
        in_specs=[ALL] + hop_specs(0),
        out_specs=[UPPER, LOWER],
        out_shape=[jax.ShapeDtypeStruct((512, 512), BF16)] * 2,
        compiler_params=pltpu.CompilerParams(vmem_limit_bytes=VMEM),
        cost_estimate=TINY,
    )(full, *hops)


def product_kernel(full_ref, *refs):
    refs[4][...] = multiply(full_ref, refs[:4])


def product(full, hops):
    return pl.pallas_call(
        product_kernel,
        grid=(4,),
        in_specs=[ALL] + hop_specs(1),
        out_specs=ROWS,
        out_shape=jax.ShapeDtypeStruct((1024, 512), F32),
        compiler_params=pltpu.CompilerParams(vmem_limit_bytes=VMEM),
        cost_estimate=TINY,
    )(full, *hops)


def closing_kernel(flags_ref, part_ref, core0_ref, core1_ref, chip0_ref, chip1_ref, sum_ref, more_ref, o_ref):
    step = pl.program_id(0)
    core = jnp.where(step == 0, core0_ref[...], core1_ref[...])
    chip = jnp.where(step == 0, chip0_ref[...], chip1_ref[...])
    for block in range(4):
        rows = slice(TILE * block, TILE * (block + 1))
        total = part_ref[rows, :] + core[rows, :].astype(F32)
        total += chip[rows, :].astype(F32)
        line = pl.ds(4 * step + block, 1)
        scale = jnp.float32(TILE * 256) / (1.0 + sum_ref[line, :] + more_ref[line, :])
        total *= jnp.transpose(jnp.broadcast_to(scale, (8, TILE)))[:, 0:1]
        for p in range(4):
            lanes = slice(TILE * p, TILE * (p + 1))
            on = flags_ref[4 * step + block, p] != 0
            o_ref[rows, lanes] = jnp.where(on, total[:, lanes], 0.0).astype(BF16)


def closing(flags, part, core, chip, sums, more):
    rows = pl.BlockSpec((512, 512), lambda i, f: (i, 0))
    side = pl.BlockSpec((8, TILE), lambda i, f: (0, 0))
    whole = pl.BlockSpec((512, 512), lambda i, f: (0, 0))
    return pl.pallas_call(
        closing_kernel,
        grid_spec=pltpu.PrefetchScalarGridSpec(
            num_scalar_prefetch=1,
            grid=(2,),
            in_specs=[rows, whole, whole, whole, whole, side, side],
            out_specs=rows,
        ),
        out_shape=jax.ShapeDtypeStruct((1024, 512), BF16),
        compiler_params=pltpu.CompilerParams(vmem_limit_bytes=VMEM),
        cost_estimate=TINY,
    )(flags, part, *core, *chip, sums, more)


class Order:
    def __init__(self):
        self.seen = []

    def send(self, value, axes, pairs):
        others = [v for v in self.seen[-5:] if v is not value]
        if others:
            value = lax.optimization_barrier((value, *others))[0]
        return lax.ppermute(value, axes, pairs)

    def wait(self, *values):
        self.seen.extend(values)


def shards(a_weights, a_flags, b_weights, b_flags, out_flags):
    rep = lax.axis_index("rep").astype(jnp.int32)
    row = lax.axis_index("row").astype(jnp.int32)
    col = lax.axis_index("col").astype(jnp.int32)
    place = jnp.stack([col >> 2, row, col & 3, rep])
    b, bf = b_weights[0], b_flags[0]
    order = Order()

    def both(v, axis, tables):
        return order.send(v, axis, tables[1]), order.send(v, axis, tables[3])

    def onward(r, l, axis, tables):
        n = r.shape[0] // 2
        return order.send(r[:n], axis, tables[1]), order.send(l[n:], axis, tables[3])

    def send_y(v, h=1):
        return order.send(v, ("row", "rep"), ALONG_Y[h])

    a, a_sum = mask(a_flags[0, :, 0], a_weights[0])
    zr, zl = both(a, "col", ALONG_Z)
    b, a = lax.optimization_barrier((b, a))
    b32, sum32 = prep(place, bf, b, 3)
    h32 = [b32, send_y(b32)]
    b10, sum10 = prep(place, bf, lax.optimization_barrier((b, sum32))[0], 1)
    h10 = [b10, send_y(b10)]
    b_sum = sum32[0] + sum32[1] + sum10[0] + sum10[1]
    total = jnp.concatenate([a_sum[:, 0, :], b_sum[:, 0, :]], 0)
    other = order.send(total, "col", COLS[4])
    order.wait(other)
    total = total + other
    other = order.send(total, "col", COLS[8])
    order.wait(other, zr, zl)
    total = total + other
    zr2, zl2 = onward(zr, zl, "col", ALONG_Z)
    other = order.send(total, "col", COLS[1])
    wide = gather(a, zr, zl, zr2, zl2)
    order.wait(zr2, zl2, other)
    xr, xl = both(wide, "col", ALONG_X)
    h32.append(send_y(h32[1]))
    total = total + other
    order.wait(h10[1])
    other = order.send(total, "col", COLS[2])
    order.wait(h32[2], other)
    total = total + other
    walk_b = 1.0 / (1.0 + total[8:])
    others = [send_y(walk_b, h) for h in (1, 2, 3)]
    order.wait(*others)
    scale = jnp.stack([walk_b] + others, 0)
    h32.append(send_y(h32[2]))

    order.wait(xr, xl)
    xr2, xl2 = onward(xr, xl, "col", ALONG_X)
    h10.append(send_y(h10[1]))
    sums = total[:8]
    more = order.send(sums, "rep", SWAP[1])
    most = early(place, scale, (wide, xr, xl))
    sums = sums + more
    more = order.send(sums, "rep", SWAP[2])
    xr2 = lax.optimization_barrier((xr2, more))[0]
    full, top3 = opening(place, scale, most, xr2, h32, 0)
    order.wait(top3)
    top_core = order.send(top3, "rep", SWAP[1])
    full, low3 = opening(place, scale, full, xl2, h32, 1)
    order.wait(low3)
    low_core = order.send(low3, "rep", SWAP[1])
    top2 = middle(full, top_core, h32, 0)
    order.wait(top2)
    top_chip = order.send(top2, "rep", SWAP[2])
    low2 = middle(full, low_core, [lax.optimization_barrier((h32[0], top2))[0]] + h32[1:], 1)
    order.wait(low2)
    low_chip = order.send(low2, "rep", SWAP[2])
    lower = send_y(h10[2])
    hops = h10 + [lax.optimization_barrier((lower, low2))[0]]
    part1 = pieces(full, hops)
    part0 = product(full, hops)
    order.wait(part0)
    core = [order.send(v, "rep", SWAP[1]) for v in part1]
    return closing(out_flags, part0, core, (top_chip, low_chip), sums, more)


def solution(mesh):
    return jax.shard_map(
        shards,
        mesh=mesh,
        in_specs=(
            P("rep", "row", "col"),
            P("rep", "row", "col"),
            P("rep", "row", "col"),
            P("rep", "row", "col"),
            P("row", ("col", "rep")),
        ),
        out_specs=P("row", ("col", "rep")),
        check_vma=False,
    )
```

```python
import functools

import jax
import jax.numpy as jnp
from jax import lax
from jax.experimental import pallas as pl
from jax.experimental.pallas import tpu as pltpu
from jax.sharding import PartitionSpec as P

TILE = 128
F32, BF16 = jnp.float32, jnp.bfloat16
TURN = (1, -1, 1, -1)
ALONG_Y = {
    h: [(4 * y + r, 4 * ((y + h * TURN[r]) % 4) + r) for y in range(4) for r in range(4)] for h in (1, 2, 3)
}
ALONG_X = {s: [(4 * x + z, 4 * ((x + s) % 4) + z) for x in range(4) for z in range(4)] for s in (1, 3)}
ALONG_Z = {s: [(4 * x + z, 4 * x + (z + s) % 4) for x in range(4) for z in range(4)] for s in (1, 3)}
SWAP = {k: [(i, i ^ k) for i in range(4)] for k in (1, 2)}
COLS = {k: [(i, i ^ k) for i in range(16)] for k in (1, 2, 4, 8)}
VMEM = 14 << 20
WAIT = 160 << 20
PAUSE = 8 << 20
TINY = pl.CostEstimate(flops=1, bytes_accessed=1, transcendentals=0)


def prep_kernel(place_ref, flags_ref, b_ref, o_ref, sum_ref, *, first):
    ones = jnp.ones((8, 512), BF16)
    block = place_ref[3] ^ (first - pl.program_id(0))
    for j in range(4):
        z = (place_ref[2] - j) & 3
        rows = pl.ds(pl.multiple_of(z * TILE, TILE), TILE)
        tiles = []
        for p in range(4):
            on = flags_ref[z, block * 4 + p] != 0
            tiles.append(jnp.where(on, b_ref[rows, TILE * p:TILE * (p + 1)], jnp.zeros((TILE, TILE), BF16)))
        line = jnp.concatenate(tiles, 1)
        o_ref[TILE * j:TILE * (j + 1), :] = line
        sum_ref[0, z] = lax.dot_general(ones, line, (((1,), (1,)), ((), ())), preferred_element_type=F32)


def prep(place, flags, b, first):
    return pl.pallas_call(
        functools.partial(prep_kernel, first=first),
        grid_spec=pltpu.PrefetchScalarGridSpec(
            num_scalar_prefetch=2,
            grid=(2,),
            in_specs=[pl.BlockSpec((512, 512), lambda i, place, flags: (0, place[3] ^ (first - i)))],
            out_specs=[
                pl.BlockSpec((512, 512), lambda i, place, flags: (0, i)),
                pl.BlockSpec((1, 4, 8, TILE), lambda i, place, flags: (i, 0, 0, 0)),
            ],
        ),
        out_shape=[jax.ShapeDtypeStruct((512, 1024), BF16), jax.ShapeDtypeStruct((2, 4, 8, TILE), F32)],
        compiler_params=pltpu.CompilerParams(vmem_limit_bytes=VMEM),
        cost_estimate=TINY,
    )(place, flags, b)


def mask_kernel(flags_ref, a_ref, o_ref, sum_ref):
    ones = jnp.ones((8, TILE), BF16)
    for k in range(8):
        rows = slice(TILE * k, TILE * (k + 1))
        tile = jnp.where(flags_ref[k] != 0, a_ref[rows, :], jnp.zeros((TILE, TILE), BF16))
        o_ref[rows, :] = tile
        sum_ref[k] = lax.dot_general(ones, tile, (((1,), (1,)), ((), ())), preferred_element_type=F32)


def mask(flags, a):
    return pl.pallas_call(
        mask_kernel,
        grid_spec=pltpu.PrefetchScalarGridSpec(
            num_scalar_prefetch=1,
            grid=(1,),
            in_specs=[pl.BlockSpec((1024, TILE), lambda i, flags: (0, 0))],
            out_specs=[
                pl.BlockSpec((1024, TILE), lambda i, flags: (0, 0)),
                pl.BlockSpec((8, 8, TILE), lambda i, flags: (0, 0, 0)),
            ],
        ),
        out_shape=[jax.ShapeDtypeStruct((1024, TILE), BF16), jax.ShapeDtypeStruct((8, 8, TILE), F32)],
        compiler_params=pltpu.CompilerParams(vmem_limit_bytes=VMEM),
        cost_estimate=TINY,
    )(flags, a)


def gather_kernel(own_ref, r_ref, l_ref, r2_ref, l2_ref, o_ref):
    o_ref[:, :TILE] = own_ref[...]
    o_ref[:, TILE:2 * TILE] = r_ref[...]
    o_ref[:512, 2 * TILE:3 * TILE] = r2_ref[...]
    o_ref[512:, 2 * TILE:3 * TILE] = l2_ref[...]
    o_ref[:, 3 * TILE:] = l_ref[...]


def gather(own, r, l, r2, l2):
    return pl.pallas_call(
        gather_kernel,
        out_shape=jax.ShapeDtypeStruct((1024, 512), BF16),
        compiler_params=pltpu.CompilerParams(vmem_limit_bytes=VMEM),
        cost_estimate=pl.CostEstimate(flops=1, bytes_accessed=WAIT, transcendentals=0),
    )(own, r, l, r2, l2)


def slot(place_ref, s):
    return ((place_ref[1] - place_ref[0] + s) * (1 - 2 * (place_ref[3] & 1))) & 3


def scaled(place_ref, scale_ref, piece, s):
    z = place_ref[2]
    scale = [scale_ref[slot(place_ref, s), pl.ds((z - j) & 3, 1), :] for j in range(4)]
    return (piece.astype(F32) * jnp.concatenate(scale, 1)).astype(BF16)


def early_kernel(place_ref, scale_ref, own_ref, r_ref, l_ref, o_ref):
    for s, ref in ((0, own_ref), (1, r_ref), (3, l_ref)):
        o_ref[slot(place_ref, s)] = scaled(place_ref, scale_ref, ref[...], s)


SCALE = pl.BlockSpec((4, 4, TILE), lambda i, *_: (0, 0, 0))
ROWS = pl.BlockSpec((256, 512), lambda i, *_: (i, 0))
ALL = pl.BlockSpec((4, 256, 512), lambda i, *_: (0, i, 0))
UPPER = pl.BlockSpec((256, 512), lambda i, *_: (jnp.minimum(i, 1), 0))
LOWER = pl.BlockSpec((256, 512), lambda i, *_: (jnp.maximum(i - 2, 0), 0))


def early(place, scale, pieces):
    return pl.pallas_call(
        early_kernel,
        grid_spec=pltpu.PrefetchScalarGridSpec(
            num_scalar_prefetch=1,
            grid=(4,),
            in_specs=[SCALE, ROWS, ROWS, ROWS],
            out_specs=ALL,
        ),
        out_shape=jax.ShapeDtypeStruct((4, 1024, 512), BF16),
        compiler_params=pltpu.CompilerParams(vmem_limit_bytes=VMEM),
        cost_estimate=TINY,
    )(place, scale, *pieces)


def multiply(a_ref, hops):
    total = jnp.dot(a_ref[0], hops[0][...], preferred_element_type=F32)
    for h in range(1, 4):
        total += jnp.dot(a_ref[h], hops[h][...], preferred_element_type=F32)
    return total


def hop_specs(q):
    return [pl.BlockSpec((512, 512), lambda i, *_: (0, q))] * 4


def opening_kernel(place_ref, scale_ref, full_ref, piece_ref, *refs):
    hops, (last_ref, o_ref) = refs[:4], refs[4:]
    last = scaled(place_ref, scale_ref, piece_ref[...], 2)
    last_ref[0] = last
    missing = slot(place_ref, 2)
    lefts = [jnp.where(missing == h, last, full_ref[h]) for h in range(4)]
    o_ref[...] = multiply(lefts, hops).astype(BF16)


def opening(place, scale, full, piece, hops, half):
    return pl.pallas_call(
        opening_kernel,
        grid_spec=pltpu.PrefetchScalarGridSpec(
            num_scalar_prefetch=1,
            grid=(2,),
            in_specs=[SCALE, pl.BlockSpec((4, 256, 512), lambda i, *_: (0, 2 * half + i, 0)), ROWS] + hop_specs(0),
            out_specs=[
                pl.BlockSpec((1, 256, 512), lambda i, place: (slot(place, 2), 2 * half + i, 0)),
                ROWS,
            ],
        ),
        out_shape=[
            jax.ShapeDtypeStruct((4, 1024, 512), BF16),
            jax.ShapeDtypeStruct((512, 512), BF16),
        ],
        input_output_aliases={2: 0},
        compiler_params=pltpu.CompilerParams(vmem_limit_bytes=VMEM),
        cost_estimate=TINY,
    )(place, scale, full, piece, *hops)


def middle_kernel(full_ref, core_ref, *refs):
    refs[4][...] = (multiply(full_ref, refs[:4]) + core_ref[...].astype(F32)).astype(BF16)


def middle(full, core, hops, half):
    return pl.pallas_call(
        middle_kernel,
        grid=(2,),
        in_specs=[pl.BlockSpec((4, 256, 512), lambda i: (0, 2 * half + i, 0)), ROWS] + hop_specs(1),
        out_specs=ROWS,
        out_shape=jax.ShapeDtypeStruct((512, 512), BF16),
        compiler_params=pltpu.CompilerParams(vmem_limit_bytes=VMEM),
        cost_estimate=TINY,
    )(full, core, *hops)


def pair_kernel(full_ref, *refs):
    hops, (upper_ref, lower_ref, part_ref) = refs[:4], refs[4:]
    swapped = multiply(full_ref, [hop[:, :512] for hop in hops]).astype(BF16)
    for k, ref in enumerate((upper_ref, lower_ref)):

        @pl.when((pl.program_id(0) >> 1) == k)
        def _():
            ref[...] = swapped

    part_ref[...] = multiply(full_ref, [hop[:, 512:] for hop in hops])


def pair(full, hops):
    return pl.pallas_call(
        pair_kernel,
        grid=(4,),
        in_specs=[ALL] + [pl.BlockSpec((512, 1024), lambda i: (0, 0))] * 4,
        out_specs=[UPPER, LOWER, ROWS],
        out_shape=[jax.ShapeDtypeStruct((512, 512), BF16)] * 2 + [jax.ShapeDtypeStruct((1024, 512), F32)],
        compiler_params=pltpu.CompilerParams(vmem_limit_bytes=20 << 20),
        cost_estimate=TINY,
    )(full, *hops)


def closing_kernel(flags_ref, part_ref, core0_ref, core1_ref, chip0_ref, chip1_ref, sum_ref, more_ref, o_ref):
    step = pl.program_id(0)
    core = jnp.where(step == 0, core0_ref[...], core1_ref[...])
    chip = jnp.where(step == 0, chip0_ref[...], chip1_ref[...])
    for block in range(4):
        rows = slice(TILE * block, TILE * (block + 1))
        total = part_ref[rows, :] + core[rows, :].astype(F32)
        total += chip[rows, :].astype(F32)
        line = pl.ds(4 * step + block, 1)
        scale = jnp.float32(TILE * 256) / (1.0 + sum_ref[line, :] + more_ref[line, :])
        total *= jnp.transpose(jnp.broadcast_to(scale, (8, TILE)))[:, 0:1]
        for p in range(4):
            lanes = slice(TILE * p, TILE * (p + 1))
            on = flags_ref[4 * step + block, p] != 0
            o_ref[rows, lanes] = jnp.where(on, total[:, lanes], 0.0).astype(BF16)


def closing(flags, part, core, chip, sums, more):
    rows = pl.BlockSpec((512, 512), lambda i, f: (i, 0))
    side = pl.BlockSpec((8, TILE), lambda i, f: (0, 0))
    whole = pl.BlockSpec((512, 512), lambda i, f: (0, 0))
    return pl.pallas_call(
        closing_kernel,
        grid_spec=pltpu.PrefetchScalarGridSpec(
            num_scalar_prefetch=1,
            grid=(2,),
            in_specs=[rows, whole, whole, whole, whole, side, side],
            out_specs=rows,
        ),
        out_shape=jax.ShapeDtypeStruct((1024, 512), BF16),
        compiler_params=pltpu.CompilerParams(vmem_limit_bytes=VMEM),
        cost_estimate=TINY,
    )(flags, part, *core, *chip, sums, more)


class Order:
    def __init__(self):
        self.seen = []

    def send(self, value, axes, pairs):
        others = [v for v in self.seen[-5:] if v is not value]
        if others:
            value = lax.optimization_barrier((value, *others))[0]
        return lax.ppermute(value, axes, pairs)

    def wait(self, *values):
        self.seen.extend(values)


def shards(a_weights, a_flags, b_weights, b_flags, out_flags):
    rep = lax.axis_index("rep").astype(jnp.int32)
    row = lax.axis_index("row").astype(jnp.int32)
    col = lax.axis_index("col").astype(jnp.int32)
    place = jnp.stack([col >> 2, row, col & 3, rep])
    b, bf = b_weights[0], b_flags[0]
    order = Order()

    def both(v, axis, tables):
        return order.send(v, axis, tables[1]), order.send(v, axis, tables[3])

    def onward(r, l, axis, tables):
        n = r.shape[0] // 2
        return order.send(r[:n], axis, tables[1]), order.send(l[n:], axis, tables[3])

    def send_y(v, h=1):
        return order.send(v, ("row", "rep"), ALONG_Y[h])

    a, a_sum = mask(a_flags[0, :, 0], a_weights[0])
    zr, zl = both(a, "col", ALONG_Z)
    b, a = lax.optimization_barrier((b, a))
    b32, sum32 = prep(place, bf, b, 3)
    h32 = [b32, send_y(b32)]
    b10, sum10 = prep(place, bf, lax.optimization_barrier((b, sum32))[0], 1)
    h10 = [b10, send_y(b10)]
    b_sum = sum32[0] + sum32[1] + sum10[0] + sum10[1]
    total = jnp.concatenate([a_sum[:, 0, :], b_sum[:, 0, :]], 0)
    other = order.send(total, "col", COLS[4])
    order.wait(other)
    total = total + other
    other = order.send(total, "col", COLS[8])
    order.wait(other, zr, zl)
    total = total + other
    zr2, zl2 = onward(zr, zl, "col", ALONG_Z)
    other = order.send(total, "col", COLS[1])
    wide = gather(a, zr, zl, zr2, zl2)
    order.wait(zr2, zl2, other)
    xr, xl = both(wide, "col", ALONG_X)
    h32.append(send_y(h32[1]))
    total = total + other
    order.wait(h10[1])
    other = order.send(total, "col", COLS[2])
    order.wait(h32[2], other)
    total = total + other
    walk_b = 1.0 / (1.0 + total[8:])
    others = [send_y(walk_b, h) for h in (1, 2, 3)]
    order.wait(*others)
    scale = jnp.stack([walk_b] + others, 0)
    h32.append(send_y(h32[2]))

    order.wait(xr, xl)
    xr2, xl2 = onward(xr, xl, "col", ALONG_X)
    h10.append(send_y(h10[1]))
    sums = total[:8]
    more = order.send(sums, "rep", SWAP[1])
    most = early(place, scale, (wide, xr, xl))
    sums = sums + more
    more = order.send(sums, "rep", SWAP[2])
    xr2 = lax.optimization_barrier((xr2, more))[0]
    full, top3 = opening(place, scale, most, xr2, h32, 0)
    order.wait(top3)
    top_core = order.send(top3, "rep", SWAP[1])
    full, low3 = opening(place, scale, full, xl2, h32, 1)
    order.wait(low3)
    low_core = order.send(low3, "rep", SWAP[1])
    top2 = middle(full, top_core, h32, 0)
    order.wait(top2)
    top_chip = order.send(top2, "rep", SWAP[2])
    low2 = middle(full, low_core, [lax.optimization_barrier((h32[0], top2))[0]] + h32[1:], 1)
    order.wait(low2)
    low_chip = order.send(low2, "rep", SWAP[2])
    lower = send_y(h10[2])
    hops = h10 + [lax.optimization_barrier((lower, low2))[0]]
    *part1, part0 = pair(full, hops)
    core = [order.send(v, "rep", SWAP[1]) for v in part1]
    return closing(out_flags, part0, core, (top_chip, low_chip), sums, more)


def solution(mesh):
    return jax.shard_map(
        shards,
        mesh=mesh,
        in_specs=(
            P("rep", "row", "col"),
            P("rep", "row", "col"),
            P("rep", "row", "col"),
            P("rep", "row", "col"),
            P("row", ("col", "rep")),
        ),
        out_specs=P("row", ("col", "rep")),
        check_vma=False,
    )
```

```python
import functools

import jax
import jax.numpy as jnp
from jax import lax
from jax.experimental import pallas as pl
from jax.experimental.pallas import tpu as pltpu
from jax.sharding import PartitionSpec as P

TILE = 128
F32, BF16 = jnp.float32, jnp.bfloat16
TURN = (1, -1, 1, -1)
ALONG_Y = {
    h: [(4 * y + r, 4 * ((y + h * TURN[r]) % 4) + r) for y in range(4) for r in range(4)] for h in (1, 2, 3)
}
ALONG_X = {s: [(4 * x + z, 4 * ((x + s) % 4) + z) for x in range(4) for z in range(4)] for s in (1, 3)}
ALONG_Z = {s: [(4 * x + z, 4 * x + (z + s) % 4) for x in range(4) for z in range(4)] for s in (1, 3)}
SWAP = {k: [(i, i ^ k) for i in range(4)] for k in (1, 2)}
COLS = {k: [(i, i ^ k) for i in range(16)] for k in (1, 2, 4, 8)}
VMEM = 14 << 20
WAIT = 160 << 20
PAUSE = 8 << 20
TINY = pl.CostEstimate(flops=1, bytes_accessed=1, transcendentals=0)


def prep_kernel(place_ref, flags_ref, b_ref, o_ref, sum_ref, *, first):
    ones = jnp.ones((8, 512), BF16)
    block = place_ref[3] ^ (first - pl.program_id(0))
    for j in range(4):
        z = (place_ref[2] - j) & 3
        rows = pl.ds(pl.multiple_of(z * TILE, TILE), TILE)
        tiles = []
        for p in range(4):
            on = flags_ref[z, block * 4 + p] != 0
            tiles.append(jnp.where(on, b_ref[rows, TILE * p:TILE * (p + 1)], jnp.zeros((TILE, TILE), BF16)))
        line = jnp.concatenate(tiles, 1)
        o_ref[TILE * j:TILE * (j + 1), :] = line
        sum_ref[0, z] = lax.dot_general(ones, line, (((1,), (1,)), ((), ())), preferred_element_type=F32)


def prep(place, flags, b, first):
    return pl.pallas_call(
        functools.partial(prep_kernel, first=first),
        grid_spec=pltpu.PrefetchScalarGridSpec(
            num_scalar_prefetch=2,
            grid=(2,),
            in_specs=[pl.BlockSpec((512, 512), lambda i, place, flags: (0, place[3] ^ (first - i)))],
            out_specs=[
                pl.BlockSpec((512, 512), lambda i, place, flags: (0, i)),
                pl.BlockSpec((1, 4, 8, TILE), lambda i, place, flags: (i, 0, 0, 0)),
            ],
        ),
        out_shape=[jax.ShapeDtypeStruct((512, 1024), BF16), jax.ShapeDtypeStruct((2, 4, 8, TILE), F32)],
        compiler_params=pltpu.CompilerParams(vmem_limit_bytes=VMEM),
        cost_estimate=TINY,
    )(place, flags, b)


def mask_kernel(flags_ref, a_ref, o_ref, sum_ref):
    ones = jnp.ones((8, TILE), BF16)
    for k in range(8):
        rows = slice(TILE * k, TILE * (k + 1))
        tile = jnp.where(flags_ref[k] != 0, a_ref[rows, :], jnp.zeros((TILE, TILE), BF16))
        o_ref[rows, :] = tile
        sum_ref[k] = lax.dot_general(ones, tile, (((1,), (1,)), ((), ())), preferred_element_type=F32)


def mask(flags, a):
    return pl.pallas_call(
        mask_kernel,
        grid_spec=pltpu.PrefetchScalarGridSpec(
            num_scalar_prefetch=1,
            grid=(1,),
            in_specs=[pl.BlockSpec((1024, TILE), lambda i, flags: (0, 0))],
            out_specs=[
                pl.BlockSpec((1024, TILE), lambda i, flags: (0, 0)),
                pl.BlockSpec((8, 8, TILE), lambda i, flags: (0, 0, 0)),
            ],
        ),
        out_shape=[jax.ShapeDtypeStruct((1024, TILE), BF16), jax.ShapeDtypeStruct((8, 8, TILE), F32)],
        compiler_params=pltpu.CompilerParams(vmem_limit_bytes=VMEM),
        cost_estimate=TINY,
    )(flags, a)


def gather_kernel(own_ref, r_ref, l_ref, r2_ref, l2_ref, o_ref):
    o_ref[:, :TILE] = own_ref[...]
    o_ref[:, TILE:2 * TILE] = r_ref[...]
    o_ref[:512, 2 * TILE:3 * TILE] = r2_ref[...]
    o_ref[512:, 2 * TILE:3 * TILE] = l2_ref[...]
    o_ref[:, 3 * TILE:] = l_ref[...]


def gather(own, r, l, r2, l2):
    return pl.pallas_call(
        gather_kernel,
        out_shape=jax.ShapeDtypeStruct((1024, 512), BF16),
        compiler_params=pltpu.CompilerParams(vmem_limit_bytes=VMEM),
        cost_estimate=pl.CostEstimate(flops=1, bytes_accessed=WAIT, transcendentals=0),
    )(own, r, l, r2, l2)


def slot(place_ref, s):
    return ((place_ref[1] - place_ref[0] + s) * (1 - 2 * (place_ref[3] & 1))) & 3


def scaled(place_ref, scale_ref, piece, s):
    z = place_ref[2]
    scale = [scale_ref[slot(place_ref, s), pl.ds((z - j) & 3, 1), :] for j in range(4)]
    return (piece.astype(F32) * jnp.concatenate(scale, 1)).astype(BF16)


def early_kernel(place_ref, scale_ref, own_ref, r_ref, l_ref, o_ref):
    for s, ref in ((0, own_ref), (1, r_ref), (3, l_ref)):
        o_ref[slot(place_ref, s)] = scaled(place_ref, scale_ref, ref[...], s)


SCALE = pl.BlockSpec((4, 4, TILE), lambda i, *_: (0, 0, 0))
ROWS = pl.BlockSpec((256, 512), lambda i, *_: (i, 0))
ALL = pl.BlockSpec((4, 256, 512), lambda i, *_: (0, i, 0))
UPPER = pl.BlockSpec((256, 512), lambda i, *_: (jnp.minimum(i, 1), 0))
LOWER = pl.BlockSpec((256, 512), lambda i, *_: (jnp.maximum(i - 2, 0), 0))


def early(place, scale, pieces):
    return pl.pallas_call(
        early_kernel,
        grid_spec=pltpu.PrefetchScalarGridSpec(
            num_scalar_prefetch=1,
            grid=(4,),
            in_specs=[SCALE, ROWS, ROWS, ROWS],
            out_specs=ALL,
        ),
        out_shape=jax.ShapeDtypeStruct((4, 1024, 512), BF16),
        compiler_params=pltpu.CompilerParams(vmem_limit_bytes=VMEM),
        cost_estimate=TINY,
    )(place, scale, *pieces)


def multiply(a_ref, hops):
    total = jnp.dot(a_ref[0], hops[0][...], preferred_element_type=F32)
    for h in range(1, 4):
        total += jnp.dot(a_ref[h], hops[h][...], preferred_element_type=F32)
    return total


def hop_specs(q):
    return [pl.BlockSpec((512, 512), lambda i, *_: (0, q))] * 4


def opening_kernel(place_ref, scale_ref, full_ref, piece_ref, *refs):
    hops, (last_ref, o_ref) = refs[:4], refs[4:]
    last = scaled(place_ref, scale_ref, piece_ref[...], 2)
    last_ref[0] = last
    missing = slot(place_ref, 2)
    lefts = [jnp.where(missing == h, last, full_ref[h]) for h in range(4)]
    o_ref[...] = multiply(lefts, hops).astype(BF16)


def opening(place, scale, full, piece, hops, half):
    return pl.pallas_call(
        opening_kernel,
        grid_spec=pltpu.PrefetchScalarGridSpec(
            num_scalar_prefetch=1,
            grid=(2,),
            in_specs=[SCALE, pl.BlockSpec((4, 256, 512), lambda i, *_: (0, 2 * half + i, 0)), ROWS] + hop_specs(0),
            out_specs=[
                pl.BlockSpec((1, 256, 512), lambda i, place: (slot(place, 2), 2 * half + i, 0)),
                ROWS,
            ],
        ),
        out_shape=[
            jax.ShapeDtypeStruct((4, 1024, 512), BF16),
            jax.ShapeDtypeStruct((512, 512), BF16),
        ],
        input_output_aliases={2: 0},
        compiler_params=pltpu.CompilerParams(vmem_limit_bytes=VMEM),
        cost_estimate=TINY,
    )(place, scale, full, piece, *hops)


def middle_kernel(full_ref, core_ref, *refs):
    refs[4][...] = (multiply(full_ref, refs[:4]) + core_ref[...].astype(F32)).astype(BF16)


def middle(full, core, hops, half):
    return pl.pallas_call(
        middle_kernel,
        grid=(2,),
        in_specs=[pl.BlockSpec((4, 256, 512), lambda i: (0, 2 * half + i, 0)), ROWS] + hop_specs(1),
        out_specs=ROWS,
        out_shape=jax.ShapeDtypeStruct((512, 512), BF16),
        compiler_params=pltpu.CompilerParams(vmem_limit_bytes=VMEM),
        cost_estimate=TINY,
    )(full, core, *hops)


def pair_kernel(full_ref, *refs):
    hops, (upper_ref, lower_ref, part_ref) = refs[:4], refs[4:]
    swapped = multiply(full_ref, [hop[:, :512] for hop in hops]).astype(BF16)
    for k, ref in enumerate((upper_ref, lower_ref)):

        @pl.when((pl.program_id(0) >> 1) == k)
        def _():
            ref[...] = swapped

    part_ref[...] = multiply(full_ref, [hop[:, 512:] for hop in hops]).astype(BF16)


def pair(full, hops):
    return pl.pallas_call(
        pair_kernel,
        grid=(4,),
        in_specs=[ALL] + [pl.BlockSpec((512, 1024), lambda i: (0, 0))] * 4,
        out_specs=[UPPER, LOWER, ROWS],
        out_shape=[jax.ShapeDtypeStruct((512, 512), BF16)] * 2 + [jax.ShapeDtypeStruct((1024, 512), BF16)],
        compiler_params=pltpu.CompilerParams(vmem_limit_bytes=20 << 20),
        cost_estimate=TINY,
    )(full, *hops)


def closing_kernel(flags_ref, part_ref, core0_ref, core1_ref, chip0_ref, chip1_ref, sum_ref, more_ref, o_ref):
    step = pl.program_id(0)
    core = jnp.where(step == 0, core0_ref[...], core1_ref[...])
    chip = jnp.where(step == 0, chip0_ref[...], chip1_ref[...])
    for block in range(4):
        rows = slice(TILE * block, TILE * (block + 1))
        total = part_ref[rows, :].astype(F32) + core[rows, :].astype(F32)
        total += chip[rows, :].astype(F32)
        line = pl.ds(4 * step + block, 1)
        scale = jnp.float32(TILE * 256) / (1.0 + sum_ref[line, :] + more_ref[line, :])
        total *= jnp.transpose(jnp.broadcast_to(scale, (8, TILE)))[:, 0:1]
        for p in range(4):
            lanes = slice(TILE * p, TILE * (p + 1))
            on = flags_ref[4 * step + block, p] != 0
            o_ref[rows, lanes] = jnp.where(on, total[:, lanes], 0.0).astype(BF16)


def closing(flags, part, core, chip, sums, more):
    rows = pl.BlockSpec((512, 512), lambda i, f: (i, 0))
    side = pl.BlockSpec((8, TILE), lambda i, f: (0, 0))
    whole = pl.BlockSpec((512, 512), lambda i, f: (0, 0))
    return pl.pallas_call(
        closing_kernel,
        grid_spec=pltpu.PrefetchScalarGridSpec(
            num_scalar_prefetch=1,
            grid=(2,),
            in_specs=[rows, whole, whole, whole, whole, side, side],
            out_specs=rows,
        ),
        out_shape=jax.ShapeDtypeStruct((1024, 512), BF16),
        compiler_params=pltpu.CompilerParams(vmem_limit_bytes=VMEM),
        cost_estimate=TINY,
    )(flags, part, *core, *chip, sums, more)


class Order:
    def __init__(self):
        self.seen = []

    def send(self, value, axes, pairs):
        others = [v for v in self.seen[-5:] if v is not value]
        if others:
            value = lax.optimization_barrier((value, *others))[0]
        return lax.ppermute(value, axes, pairs)

    def wait(self, *values):
        self.seen.extend(values)


def shards(a_weights, a_flags, b_weights, b_flags, out_flags):
    rep = lax.axis_index("rep").astype(jnp.int32)
    row = lax.axis_index("row").astype(jnp.int32)
    col = lax.axis_index("col").astype(jnp.int32)
    place = jnp.stack([col >> 2, row, col & 3, rep])
    b, bf = b_weights[0], b_flags[0]
    order = Order()

    def both(v, axis, tables):
        return order.send(v, axis, tables[1]), order.send(v, axis, tables[3])

    def onward(r, l, axis, tables):
        n = r.shape[0] // 2
        return order.send(r[:n], axis, tables[1]), order.send(l[n:], axis, tables[3])

    def send_y(v, h=1):
        return order.send(v, ("row", "rep"), ALONG_Y[h])

    a, a_sum = mask(a_flags[0, :, 0], a_weights[0])
    zr, zl = both(a, "col", ALONG_Z)
    b, a = lax.optimization_barrier((b, a))
    b32, sum32 = prep(place, bf, b, 3)
    h32 = [b32, send_y(b32)]
    b10, sum10 = prep(place, bf, lax.optimization_barrier((b, sum32))[0], 1)
    h10 = [b10, send_y(b10)]
    b_sum = sum32[0] + sum32[1] + sum10[0] + sum10[1]
    total = jnp.concatenate([a_sum[:, 0, :], b_sum[:, 0, :]], 0)
    other = order.send(total, "col", COLS[4])
    order.wait(other)
    total = total + other
    other = order.send(total, "col", COLS[8])
    order.wait(other, zr, zl)
    total = total + other
    zr2, zl2 = onward(zr, zl, "col", ALONG_Z)
    other = order.send(total, "col", COLS[1])
    wide = gather(a, zr, zl, zr2, zl2)
    order.wait(zr2, zl2, other)
    xr, xl = both(wide, "col", ALONG_X)
    h32.append(send_y(h32[1]))
    total = total + other
    order.wait(h10[1])
    other = order.send(total, "col", COLS[2])
    order.wait(h32[2], other)
    total = total + other
    walk_b = 1.0 / (1.0 + total[8:])
    others = [send_y(walk_b, h) for h in (1, 2, 3)]
    order.wait(*others)
    scale = jnp.stack([walk_b] + others, 0)
    h32.append(send_y(h32[2]))

    order.wait(xr, xl)
    xr2, xl2 = onward(xr, xl, "col", ALONG_X)
    h10.append(send_y(h10[1]))
    sums = total[:8]
    more = order.send(sums, "rep", SWAP[1])
    most = early(place, scale, (wide, xr, xl))
    sums = sums + more
    more = order.send(sums, "rep", SWAP[2])
    xr2 = lax.optimization_barrier((xr2, more))[0]
    full, top3 = opening(place, scale, most, xr2, h32, 0)
    order.wait(top3)
    top_core = order.send(top3, "rep", SWAP[1])
    full, low3 = opening(place, scale, full, xl2, h32, 1)
    order.wait(low3)
    low_core = order.send(low3, "rep", SWAP[1])
    top2 = middle(full, top_core, h32, 0)
    order.wait(top2)
    top_chip = order.send(top2, "rep", SWAP[2])
    low2 = middle(full, low_core, [lax.optimization_barrier((h32[0], top2))[0]] + h32[1:], 1)
    order.wait(low2)
    low_chip = order.send(low2, "rep", SWAP[2])
    lower = send_y(h10[2])
    hops = h10 + [lax.optimization_barrier((lower, low2))[0]]
    *part1, part0 = pair(full, hops)
    core = [order.send(v, "rep", SWAP[1]) for v in part1]
    return closing(out_flags, part0, core, (top_chip, low_chip), sums, more)


def solution(mesh):
    return jax.shard_map(
        shards,
        mesh=mesh,
        in_specs=(
            P("rep", "row", "col"),
            P("rep", "row", "col"),
            P("rep", "row", "col"),
            P("rep", "row", "col"),
            P("row", ("col", "rep")),
        ),
        out_specs=P("row", ("col", "rep")),
        check_vma=False,
    )
```
